128 devices in a mesh: node: 4 (over z_hi, core), wide: 32 (over z_lo, y, x).
Axes of the slice: x: 4, y: 4, z: 4 (z_hi: 2, z_lo: 2; z = z_hi * 2 + z_lo), core: 2. Of those that a mesh axis runs over, the one named last changes fastest.
Arguments:
- tokens: bfloat16 [8192, 4096], P(('node', 'wide')), may hold values from -6 to 6
- expert_ids: int32 [8192, 6], P(('node', 'wide')), may hold values from 0 to 127, all different within a row; in each aligned block of 64 rows (0 to 63, 64 to 127, ...) at most 4 rows name the same one
- gate_weights: float32 [8192, 6], P(('node', 'wide')), may hold values from 0.1 to 1
- w_gate: bfloat16 [128, 4096, 768], P(('node', 'wide')), may hold values from -0.09375 to 0.09375
- w_up: bfloat16 [128, 4096, 768], P(('node', 'wide')), may hold values from -0.09375 to 0.09375
- w_down: bfloat16 [128, 768, 4096], P(('node', 'wide')), may hold values from -0.21875 to 0.21875
- gate_scale: float32 [128, 768], P(('node', 'wide')), may hold values from 0.5 to 2
- up_scale: float32 [128, 768], P(('node', 'wide')), may hold values from 0.5 to 2
- down_scale: float32 [128, 4096], P(('node', 'wide')), may hold values from 0.5 to 2
Outputs:
- mixed: bfloat16 [8192, 4096], P(('node', 'wide'))
The draws below stay inside these ranges and needn't reach their ends.
Inputs may be any that keep to these rules, and one draw needn't show every extreme that they name: `expert_ids`: each token names 6 different experts; among the routes of the tokens of one device no expert is named more than 4 times, a bound that some block reaches.
All inputs are finite; a program needn't handle non-finite values.
Results may differ from the reference program's by a relative error of at most 0.0058.
Values may be sent and summed in bfloat16 or wider, within the bound.
No kernel may reach another device: no remote copies, remote signals or barrier semaphores. Data moves between devices by JAX's collectives and lax.ppermute only.
A program may use at most 128 MiB of HBM per device.

```python
import math
import jax
import jax.numpy as jnp
import numpy as np
from jax import lax

D = 4096
TOP = 6
FFW = 768
TOK_DEV = 64
EXPERTS = 128
TOKENS = 8192
CAP = 4


def block_levels(stream_key, dims, cuts, smallest, largest):
    def one(dim, parts):
        draws = jax.random.uniform(jax.random.fold_in(jax.random.fold_in(stream_key, 6), dim), (parts,), jnp.float32, smallest / len(cuts), largest / len(cuts))
        return jnp.repeat(jnp.exp(draws), dims[dim] // parts).reshape((-1,) + (1,) * (len(dims) - dim - 1))

    loudness = one(*cuts[0])
    for cut in cuts[1:]:
        loudness = loudness * one(*cut)
    return loudness


def assign_block(key, own, number, rows, amount, top, most, slope):
    order = jax.random.permutation(key, amount)
    packed, ordinary = load_shares(amount, rows * top, most, slope, True), load_shares(amount, rows * top, most, slope, False)
    places = jnp.arange(amount)

    def named(tallies, offset_by):
        used = int((tallies > 0).sum())
        fixed = max(1, used // 4)
        shifted = fixed + (places - fixed + offset_by * (used - fixed)) % max(1, amount - fixed)
        return jnp.zeros((amount,), jnp.int32).at[order[jnp.where(places < fixed, places, shifted)]].set(jnp.asarray(tallies, jnp.int32))

    tallies = jnp.where(number % 4 == 0, named(packed, number // 4), named(ordinary, number - number // 4 - 1))
    mixed = jax.random.permutation(jax.random.fold_in(own, 3), amount)
    source_of, taker = mixed[0:amount // 2 * 2:2], mixed[1:amount // 2 * 2:2]
    margin = jnp.minimum(tallies[source_of] - 1, most - tallies[taker]) // 2
    margin = jnp.where((source_of == order[0]) | (taker == order[0]) | (tallies[taker] == 0), 0, jnp.maximum(margin, 0))
    shifted = jax.random.randint(jax.random.fold_in(own, 4), (amount // 2,), 0, 1 << 20) % (margin + 1)
    tallies = tallies.at[source_of].add(-shifted).at[taker].add(shifted)
    labels = jnp.searchsorted(jnp.cumsum(tallies), jnp.arange(rows * top), side="right").astype(jnp.int32)
    grid = labels.reshape(top, rows).T
    grid = grid[jax.random.permutation(jax.random.fold_in(own, 1), rows)]
    offset_by = jax.random.randint(jax.random.fold_in(own, 2), (rows, 1), 0, top)
    return jnp.take_along_axis(grid, (jnp.arange(top)[None, :] + offset_by) % top, axis=1)


def load_shares(number_of, total, most, slope, full):
    weights = [(1 << 20) // math.isqrt(grade ** slope) + 1 for grade in range(1, number_of + 1)]
    largest = most if full else min(most, max(-(-total // number_of), total * weights[0] // sum(weights)))
    least = 1 if total - largest >= number_of - 1 else 0
    counts, surplus = [largest] + [least] * (number_of - 1), total - largest - least * (number_of - 1)
    while surplus > 0:
        free = [i for i in range(1, number_of) if counts[i] < largest] or [i for i in range(1, number_of) if counts[i] < most]
        pool, left = sum([weights[i] for i in free]), surplus
        for i in free:
            addition = min(most - counts[i], max(1, left * weights[i] // pool), surplus)
            counts[i] = counts[i] + addition
            surplus = surplus - addition
    return np.array(counts)


def centred(own_key, dims, deviation, most, pieces=(), kind=jnp.bfloat16):
    level = block_levels(own_key, dims, pieces, -0.22, 0.18) if pieces else 1.0
    values = jax.random.normal(own_key, dims, jnp.float32) * deviation * level
    return jnp.minimum(jnp.maximum(values, -most), most).astype(kind)


def setup_inputs(seed: int = 0) -> dict:
    key_of = jax.random.split(jax.random.key(seed), 10)
    tokens = centred(key_of[0], (TOKENS, D), 1.0, 6.0, ((0, 128),))
    expert_ids_keys = jax.random.split(jax.random.fold_in(key_of[1], 1), TOKENS // TOK_DEV)
    expert_ids_turns = jax.random.permutation(jax.random.fold_in(key_of[1], 3), TOKENS // TOK_DEV)
    expert_ids = jax.vmap(lambda own, number: assign_block(jax.random.fold_in(key_of[1], 2), own, number, TOK_DEV, EXPERTS, TOP, CAP, 2))(expert_ids_keys, expert_ids_turns).reshape((TOKENS, TOP))
    gate_weights = jnp.clip(0.1 + 0.9 * jax.random.uniform(key_of[2], (TOKENS, TOP), jnp.float32) ** block_levels(key_of[2], (TOKENS, TOP), ((0, 128),), -0.2, 0.2), 0.1, 1.0)
    w_gate = centred(key_of[3], (EXPERTS, D, FFW), D ** -0.5, 0.09375, ((0, 128),))
    w_up = centred(key_of[4], (EXPERTS, D, FFW), D ** -0.5, 0.09375, ((0, 128),))
    w_down = centred(key_of[5], (EXPERTS, FFW, D), FFW ** -0.5, 0.21875, ((0, 128),))
    gate_scale = jnp.clip(jnp.exp(math.log(2.0) - 1.3862944 * jax.random.uniform(key_of[6], (EXPERTS, FFW), jnp.float32) ** block_levels(key_of[6], (EXPERTS, FFW), ((0, 128),), -0.2, 0.2)), 0.5, 2.0)
    up_scale = jnp.clip(jnp.exp(math.log(2.0) - 1.3862944 * jax.random.uniform(key_of[7], (EXPERTS, FFW), jnp.float32) ** block_levels(key_of[7], (EXPERTS, FFW), ((0, 128),), -0.2, 0.2)), 0.5, 2.0)
    down_scale = jnp.clip(jnp.exp(math.log(2.0) - 1.3862944 * jax.random.uniform(key_of[8], (EXPERTS, D), jnp.float32) ** block_levels(key_of[8], (EXPERTS, D), ((0, 128),), -0.2, 0.2)), 0.5, 2.0)
    return dict(tokens=tokens, expert_ids=expert_ids, gate_weights=gate_weights, w_gate=w_gate, w_up=w_up, w_down=w_down, gate_scale=gate_scale, up_scale=up_scale, down_scale=down_scale)


def reference(tokens, expert_ids, gate_weights, w_gate, w_up, w_down, gate_scale, up_scale, down_scale):
    blocks = TOKENS // TOK_DEV
    block_ids = expert_ids.reshape(blocks, TOK_DEV * TOP)
    onehot = (block_ids[:, :, None] == jnp.arange(EXPERTS, dtype=jnp.int32)[None, None, :]).astype(jnp.int32)
    before = jnp.cumsum(onehot, axis=1) - onehot
    position = jnp.sum(before * onehot, axis=2).astype(jnp.int32)
    slot_rows = (jnp.arange(blocks, dtype=jnp.int32)[:, None] * CAP + position).reshape(-1).astype(jnp.int32)
    flat_ids = expert_ids.reshape(-1).astype(jnp.int32)
    token_of = (jnp.arange(TOKENS * TOP, dtype=jnp.int32) // TOP).astype(jnp.int32)
    table = jnp.full((EXPERTS, blocks * CAP), TOKENS, jnp.int32).at[flat_ids, slot_rows].set(token_of)
    weight_of = jnp.zeros((EXPERTS, blocks * CAP), jnp.float32).at[flat_ids, slot_rows].set(gate_weights.reshape(-1))
    padded = jnp.concatenate([tokens, jnp.zeros((1, D), jnp.bfloat16)], axis=0)

    def one_expert(total, inputs):
        index, weight, g_mat, u_mat, d_mat, g_scale, u_scale, d_scale = inputs
        rows = padded[index]
        gate = jnp.dot(rows, g_mat, preferred_element_type=jnp.float32) * g_scale
        up = jnp.dot(rows, u_mat, preferred_element_type=jnp.float32) * u_scale
        hidden = (jax.nn.silu(gate) * up).astype(jnp.bfloat16)
        routed = (jnp.dot(hidden, d_mat, preferred_element_type=jnp.float32) * d_scale).astype(jnp.bfloat16)
        total = total.at[index].add(weight[:, None] * routed.astype(jnp.float32), mode="drop")
        return total, None

    start = jnp.zeros((TOKENS, D), jnp.float32)
    total, unused = lax.scan(one_expert, start, (table, weight_of, w_gate, w_up, w_down, gate_scale, up_scale, down_scale))
    return total.astype(jnp.bfloat16)
```

```python
import functools

import jax
import jax.numpy as jnp
from jax import lax
from jax.experimental import pallas as pl
from jax.experimental.pallas import tpu as pltpu
from jax.sharding import PartitionSpec as P

AXES = ("node", "wide")
BF = jnp.bfloat16
F32 = jnp.float32
MIB = 1 << 20


def iota(shape, dim):
    return lax.broadcasted_iota(jnp.int32, shape, dim)


def onehot(mask):
    return jnp.where(mask, 1.0, 0.0).astype(BF)


def dot(a, b, dims=((1,), (0,))):
    return lax.dot_general(a, b, (dims, ((), ())), preferred_element_type=F32)


def codes(ids, experts):
    top, count = ids.shape
    named = jnp.zeros((experts, count), F32)
    for k in range(top):
        named = named + jnp.where(iota((experts, count), 0) == ids[k : k + 1, :], 1.0, 0.0)
    named = named.astype(BF)
    lane = iota((count, 2 * count), 1) % count
    row = iota((count, 2 * count), 0)
    position = dot(named, onehot(row < lane))
    twice = dot(named, onehot(row == lane))
    return (position + 8.0 * (1.0 - twice)).astype(BF)


def pack_body(ids_ref, low_ref, high_ref, out_ref, hot_ref, *, experts, slots):
    count = low_ref.shape[0]
    rows = experts * 2 * slots

    @pl.when(pl.program_id(0) == 0)
    def _():
        code = codes(ids_ref[...], experts)
        spread = onehot(iota((rows, experts), 0) // (2 * slots) == iota((rows, experts), 1))
        wide = dot(spread, code)
        shape = (rows, 2 * count)
        slot = (iota(shape, 0) % slots).astype(F32)
        half = iota(shape, 0) // slots % 2
        hot_ref[...] = onehot((wide == slot) & (half == iota(shape, 1) // count))

    stacked = jnp.concatenate([low_ref[...], high_ref[...]], axis=0)
    out_ref[...] = dot(hot_ref[...], stacked).astype(BF)


def pack(ids, tokens, experts, slots, steps=4):
    top, count = ids.shape
    half = tokens.shape[1] // 2
    width = half // steps
    rows = experts * 2 * slots
    return pl.pallas_call(
        functools.partial(pack_body, experts=experts, slots=slots),
        out_shape=jax.ShapeDtypeStruct((rows, half), BF),
        grid=(steps,),
        in_specs=[
            pl.BlockSpec((top, count), lambda i: (0, 0)),
            pl.BlockSpec((count, width), lambda i: (0, i)),
            pl.BlockSpec((count, width), lambda i: (0, i + steps)),
        ],
        out_specs=pl.BlockSpec((rows, width), lambda i: (0, i)),
        scratch_shapes=[pltpu.VMEM((rows, 2 * count), BF)],
        compiler_params=pltpu.CompilerParams(vmem_limit_bytes=24 * MIB),
        name="pack",
    )(ids, tokens, tokens)


def mixer_body(ids_ref, weights_ref, out_ref, *, experts, slots):
    ids, weights = ids_ref[...], weights_ref[...]
    top, count = ids.shape
    rows = experts * 2 * slots
    code = codes(ids, experts)
    chosen = jnp.zeros((experts, count), F32)
    for k in range(top):
        chosen = chosen + jnp.where(iota((experts, count), 0) == ids[k : k + 1, :], weights[k : k + 1, :], 0.0)
    twice = onehot(iota((count, 2 * count), 0) == iota((count, 2 * count), 1) % count)
    spread = onehot(iota((experts, rows), 1) // (2 * slots) == iota((experts, rows), 0))
    shape = (2 * count, rows)
    wide = dot(code, spread, ((0,), (0,)))
    slot = (iota(shape, 1) % slots).astype(F32)
    here = (wide == slot) & (iota(shape, 1) // slots % 2 == iota(shape, 0) // count)
    high = chosen.astype(BF)
    low = (chosen - high.astype(F32)).astype(BF)
    for n, part in enumerate((high, low)):
        part = dot(part, twice).astype(BF)
        part = dot(part, spread, ((0,), (0,)))
        out_ref[n * 2 * count : (n + 1) * 2 * count, :] = jnp.where(here, part, 0.0).astype(BF)


def mixer(ids, weights, experts, slots):
    count = ids.shape[1]
    return pl.pallas_call(
        functools.partial(mixer_body, experts=experts, slots=slots),
        out_shape=jax.ShapeDtypeStruct((4 * count, experts * 2 * slots), BF),
        compiler_params=pltpu.CompilerParams(vmem_limit_bytes=24 * MIB),
        name="mixer",
    )(ids, weights)


def expert_body(
    x_hbm, gate_hbm, up_hbm, down_hbm, gate_s, up_s, down_s, out_hbm,
    x_buf, g_buf, u_buf, d_buf, xs, hid, o_buf, x_sem, g_sem, u_sem, d_sem, o_sem,
    *, slots, nb, cb,
):
    rows, half = x_hbm.shape
    ffw = gate_s.shape[1]
    wn, wc = ffw // nb, half // cb
    blocks = rows // 256

    def copies():
        xc = [pltpu.make_async_copy(x_hbm.at[pl.ds(b * 256, 256)], x_buf.at[pl.ds(b * 256, 256)], x_sem.at[b]) for b in range(blocks)]
        gc = [pltpu.make_async_copy(gate_hbm.at[0, :, pl.ds(n * wn, wn)], g_buf.at[n], g_sem.at[n]) for n in range(nb)]
        uc = [pltpu.make_async_copy(up_hbm.at[0, :, pl.ds(n * wn, wn)], u_buf.at[n], u_sem.at[n]) for n in range(nb)]
        dc = [pltpu.make_async_copy(down_hbm.at[0, :, pl.ds(c * wc, wc)], d_buf.at[c], d_sem.at[c]) for c in range(2 * cb)]
        return xc, gc, uc, dc

    xc, gc, uc, dc = copies()
    for c in xc:
        c.start()
    for n in range(nb):
        gc[n].start()
        uc[n].start()
    for c in range(cb):
        dc[c].start()
        dc[cb + c].start()

    a, b = iota((256, 256), 0), iota((256, 256), 1)
    split = onehot(b == a % 128 // slots * (2 * slots) + a // 128 * slots + a % slots)
    join = onehot(a == b % 128 // slots * (2 * slots) + b // 128 * slots + b % slots)

    for n in range(blocks):
        xc[n].wait()
        part = dot(split, x_buf[n * 256 : (n + 1) * 256, :]).astype(BF)
        xs[n * 128 : (n + 1) * 128, :half] = part[:128]
        xs[n * 128 : (n + 1) * 128, half:] = part[128:]
    for n in range(nb):
        gc[n].wait()
        gate = dot(xs[...], g_buf[n]) * gate_s[:, n * wn : (n + 1) * wn]
        uc[n].wait()
        up = dot(xs[...], u_buf[n]) * up_s[:, n * wn : (n + 1) * wn]
        hid[:, n * wn : (n + 1) * wn] = (gate / (1.0 + jnp.exp(-gate)) * up).astype(BF)
    for c in range(cb):
        dc[c].wait()
        dc[cb + c].wait()
        low = (dot(hid[...], d_buf[c]) * down_s[:, c * wc : (c + 1) * wc]).astype(BF)
        high = (dot(hid[...], d_buf[cb + c]) * down_s[:, half + c * wc : half + (c + 1) * wc]).astype(BF)
        for n in range(blocks):
            both = jnp.concatenate([low[n * 128 : (n + 1) * 128], high[n * 128 : (n + 1) * 128]], axis=0)
            o_buf[c, n * 256 : (n + 1) * 256, :] = dot(join, both).astype(BF)
        pltpu.make_async_copy(o_buf.at[c], out_hbm.at[:, pl.ds(c * wc, wc)], o_sem.at[c]).start()
    for c in range(cb):
        pltpu.make_async_copy(o_buf.at[c], out_hbm.at[:, pl.ds(c * wc, wc)], o_sem.at[c]).wait()


def expert(x, w_gate, w_up, w_down, gate_scale, up_scale, down_scale, slots, nb=3, cb=4):
    rows, half = x.shape
    width, ffw = w_gate.shape[1:]
    wn, wc = ffw // nb, half // cb
    whole = pl.BlockSpec(memory_space=pltpu.VMEM)
    hbm = pl.BlockSpec(memory_space=pl.ANY)
    return pl.pallas_call(
        functools.partial(expert_body, slots=slots, nb=nb, cb=cb),
        out_shape=jax.ShapeDtypeStruct((rows, half), BF),
        in_specs=[hbm, hbm, hbm, hbm, whole, whole, whole],
        out_specs=hbm,
        scratch_shapes=[
            pltpu.VMEM((rows, half), BF),
            pltpu.VMEM((nb, width, wn), BF),
            pltpu.VMEM((nb, width, wn), BF),
            pltpu.VMEM((2 * cb, ffw, wc), BF),
            pltpu.VMEM((rows // 2, width), BF),
            pltpu.VMEM((rows // 2, ffw), BF),
            pltpu.VMEM((cb, rows, wc), BF),
            pltpu.SemaphoreType.DMA((rows // 256,)),
            pltpu.SemaphoreType.DMA((nb,)),
            pltpu.SemaphoreType.DMA((nb,)),
            pltpu.SemaphoreType.DMA((2 * cb,)),
            pltpu.SemaphoreType.DMA((cb,)),
        ],
        compiler_params=pltpu.CompilerParams(vmem_limit_bytes=56 * MIB),
        name="expert",
    )(x, w_gate, w_up, w_down, gate_scale, up_scale, down_scale)


def mix_body(w_ref, r_ref, out_ref, *, steps):
    count = w_ref.shape[0] // 4
    half = out_ref.shape[1] // 2
    width = half // steps
    both = dot(w_ref[...], r_ref[...])
    total = (both[: 2 * count] + both[2 * count :]).astype(BF)
    at = pl.multiple_of(pl.program_id(0) * width, width)
    out_ref[:, pl.ds(at, width)] = total[:count]
    out_ref[:, pl.ds(half + at, width)] = total[count:]


def mix(weights, results, steps=4):
    count = weights.shape[0] // 4
    rows, half = results.shape
    width = half // steps
    return pl.pallas_call(
        functools.partial(mix_body, steps=steps),
        out_shape=jax.ShapeDtypeStruct((count, 2 * half), BF),
        grid=(steps,),
        in_specs=[
            pl.BlockSpec(weights.shape, lambda i: (0, 0)),
            pl.BlockSpec((rows, width), lambda i: (0, i)),
        ],
        out_specs=pl.BlockSpec((count, 2 * half), lambda i: (0, 0)),
        compiler_params=pltpu.CompilerParams(vmem_limit_bytes=24 * MIB),
        name="mix",
    )(weights, results)


def exchange(x, experts):
    rows, width = x.shape
    x = x.reshape(experts, rows // experts, width)
    return lax.all_to_all(x, AXES, split_axis=0, concat_axis=0, tiled=True).reshape(rows, width)


def on_device(tokens, expert_ids, gate_weights, w_gate, w_up, w_down, gate_scale, up_scale, down_scale):
    experts = lax.axis_size(AXES)
    slots = 4
    ids, weights = expert_ids.T, gate_weights.T
    packed = pack(ids, tokens, experts, slots)
    received = exchange(packed, experts)
    routed = expert(received, w_gate, w_up, w_down, gate_scale, up_scale, down_scale, slots)
    returned = exchange(routed, experts)
    return mix(mixer(ids, weights, experts, slots), returned)


def solution(mesh):
    row = P(AXES, None)
    placed = (row, row, row, P(AXES, None, None), P(AXES, None, None), P(AXES, None, None), row, row, row)
    return jax.shard_map(on_device, mesh=mesh, in_specs=placed, out_specs=row, check_vma=False)
```

```python
import functools

import jax
import jax.numpy as jnp
from jax import lax
from jax.experimental import pallas as pl
from jax.experimental.pallas import tpu as pltpu
from jax.sharding import PartitionSpec as P

AXES = ("node", "wide")
BF = jnp.bfloat16
F32 = jnp.float32
MIB = 1 << 20


def iota(shape, dim):
    return lax.broadcasted_iota(jnp.int32, shape, dim)


def onehot(mask):
    return jnp.where(mask, 1.0, 0.0).astype(BF)


def dot(a, b, dims=((1,), (0,))):
    return lax.dot_general(a, b, (dims, ((), ())), preferred_element_type=F32)


def in_hbm(x):
    return pltpu.with_memory_space_constraint(x, pltpu.HBM)


def codes(ids, experts):
    top, count = ids.shape
    named = jnp.zeros((experts, count), F32)
    for k in range(top):
        named = named + jnp.where(iota((experts, count), 0) == ids[k : k + 1, :], 1.0, 0.0)
    named = named.astype(BF)
    lane = iota((count, 2 * count), 1) % count
    row = iota((count, 2 * count), 0)
    position = dot(named, onehot(row < lane))
    twice = dot(named, onehot(row == lane))
    return (position + 8.0 * (1.0 - twice)).astype(BF)


def pack_body(ids_hbm, tokens_hbm, out_ref, ids_ref, tok_ref, sem, *, experts, slots, steps):
    count, width = tok_ref.shape
    half = width // 2
    rows = experts * 2 * slots
    ids_copy = pltpu.make_async_copy(ids_hbm, ids_ref, sem.at[0])
    tok_copy = pltpu.make_async_copy(tokens_hbm, tok_ref, sem.at[1])
    ids_copy.start()
    tok_copy.start()
    shape = (rows, 2 * count)
    spread = onehot(iota((rows, experts), 0) // (2 * slots) == iota((rows, experts), 1))
    slot = (iota(shape, 0) % slots).astype(F32)
    half_of = iota(shape, 0) // slots % 2 == iota(shape, 1) // count
    ids_copy.wait()
    wide = dot(spread, codes(ids_ref[...], experts))
    hot = onehot((wide == slot) & half_of)
    tok_copy.wait()
    step = half // steps
    for n in range(steps):
        at = slice(n * step, (n + 1) * step)
        stacked = jnp.concatenate([tok_ref[:, at], tok_ref[:, half + n * step : half + (n + 1) * step]], axis=0)
        out_ref[:, at] = dot(hot, stacked).astype(BF)


def pack(ids, tokens, experts, slots, steps=4):
    rows = experts * 2 * slots
    hbm = pl.BlockSpec(memory_space=pltpu.HBM)
    return pl.pallas_call(
        functools.partial(pack_body, experts=experts, slots=slots, steps=steps),
        out_shape=jax.ShapeDtypeStruct((rows, tokens.shape[1] // 2), BF),
        in_specs=[hbm, hbm],
        out_specs=pl.BlockSpec(memory_space=pltpu.VMEM),
        scratch_shapes=[
            pltpu.VMEM(ids.shape, jnp.int32),
            pltpu.VMEM(tokens.shape, BF),
            pltpu.SemaphoreType.DMA((2,)),
        ],
        compiler_params=pltpu.CompilerParams(vmem_limit_bytes=12 * MIB),
        name="pack",
    )(in_hbm(ids), in_hbm(tokens))


def mixer_body(ids_ref, weights_ref, out_ref, *, experts, slots):
    ids, weights = ids_ref[...], weights_ref[...]
    top, count = ids.shape
    rows = experts * 2 * slots
    code = codes(ids, experts)
    chosen = jnp.zeros((experts, count), F32)
    for k in range(top):
        chosen = chosen + jnp.where(iota((experts, count), 0) == ids[k : k + 1, :], weights[k : k + 1, :], 0.0)
    twice = onehot(iota((count, 2 * count), 0) == iota((count, 2 * count), 1) % count)
    spread = onehot(iota((experts, rows), 1) // (2 * slots) == iota((experts, rows), 0))
    shape = (2 * count, rows)
    wide = dot(code, spread, ((0,), (0,)))
    slot = (iota(shape, 1) % slots).astype(F32)
    here = (wide == slot) & (iota(shape, 1) // slots % 2 == iota(shape, 0) // count)
    high = chosen.astype(BF)
    low = (chosen - high.astype(F32)).astype(BF)
    for n, part in enumerate((high, low)):
        part = dot(part, twice).astype(BF)
        part = dot(part, spread, ((0,), (0,)))
        out_ref[n * 2 * count : (n + 1) * 2 * count, :] = jnp.where(here, part, 0.0).astype(BF)


def mixer(ids, weights, experts, slots):
    count = ids.shape[1]
    return pl.pallas_call(
        functools.partial(mixer_body, experts=experts, slots=slots),
        out_shape=jax.ShapeDtypeStruct((4 * count, experts * 2 * slots), BF),
        compiler_params=pltpu.CompilerParams(vmem_limit_bytes=8 * MIB),
        name="mixer",
    )(ids, weights)


def swap(first, second):
    top = iota(first.shape, 1) < 4
    return (
        jnp.where(top, first, pltpu.roll(second, 4, 1)),
        jnp.where(top, pltpu.roll(first, 4, 1), second),
    )


def expert_body(
    x_ref, gate_ref, up_ref, down_hbm, gate_s, up_s, down_s, out_hbm, d_buf, xs, hid, o_buf, d_sem, o_sem, *, slots, nb, cb
):
    rows, half = x_ref.shape
    ffw = gate_s.shape[1]
    wn, wc = ffw // nb, half // cb
    blocks = rows // 256
    downs = [pltpu.make_async_copy(down_hbm.at[0, pl.ds(n * wn, wn)], d_buf.at[pl.ds(n * wn, wn)], d_sem.at[n]) for n in range(nb)]
    outs = [pltpu.make_async_copy(o_buf.at[:, pl.ds(c * wc, wc)], out_hbm.at[:, pl.ds(c * wc, wc)], o_sem.at[c]) for c in range(cb)]
    for copy in downs:
        copy.start()
    wx = 256
    for n in range(half // wx):
        at = slice(n * wx, (n + 1) * wx)
        pairs = x_ref[:, at].astype(F32).reshape(rows // 16, 2, 8, wx)
        low, high = swap(pairs[:, 0], pairs[:, 1])
        xs[:, at] = low.reshape(rows // 2, wx).astype(BF)
        xs[:, half + n * wx : half + (n + 1) * wx] = high.reshape(rows // 2, wx).astype(BF)
    for n in range(nb):
        at = slice(n * wn, (n + 1) * wn)
        gate = dot(xs[...], gate_ref[0, :, at]) * gate_s[:, at]
        up = dot(xs[...], up_ref[0, :, at]) * up_s[:, at]
        hid[:, at] = (gate / (1.0 + jnp.exp(-gate)) * up).astype(BF)
    for copy in downs:
        copy.wait()
    for c in range(cb):
        at, to = slice(c * wc, (c + 1) * wc), slice(half + c * wc, half + (c + 1) * wc)
        low = dot(hid[...], d_buf[:, at]) * down_s[:, at]
        high = dot(hid[...], d_buf[:, to]) * down_s[:, to]
        tile = (rows // 16, 8, wc)
        even, odd = swap(low.reshape(tile), high.reshape(tile))
        both = jnp.concatenate([even[:, None], odd[:, None]], axis=1)
        o_buf[:, at] = both.reshape(rows, wc).astype(BF)
        outs[c].start()
    for copy in outs:
        copy.wait()


def expert(x, w_gate, w_up, w_down, gate_scale, up_scale, down_scale, slots, nb=3, cb=4):
    rows, half = x.shape
    width, ffw = w_gate.shape[1:]
    whole = pl.BlockSpec(memory_space=pltpu.VMEM)
    hbm = pl.BlockSpec(memory_space=pltpu.HBM)
    return pl.pallas_call(
        functools.partial(expert_body, slots=slots, nb=nb, cb=cb),
        out_shape=pltpu.HBM((rows, half), BF),
        in_specs=[whole, whole, whole, hbm, whole, whole, whole],
        out_specs=hbm,
        scratch_shapes=[
            pltpu.VMEM((ffw, width), BF),
            pltpu.VMEM((rows // 2, width), BF),
            pltpu.VMEM((rows // 2, ffw), BF),
            pltpu.VMEM((rows, half), BF),
            pltpu.SemaphoreType.DMA((nb,)),
            pltpu.SemaphoreType.DMA((cb,)),
        ],
        compiler_params=pltpu.CompilerParams(vmem_limit_bytes=24 * MIB),
        name="expert",
    )(x, w_gate, w_up, in_hbm(w_down), gate_scale, up_scale, down_scale)


def mix_body(w_ref, r_hbm, out_hbm, r_buf, buf, in_sem, sem, *, steps):
    count = w_ref.shape[0] // 4
    half = r_buf.shape[1]
    step = half // steps
    here = [pl.ds(n * step, step) for n in range(2 * steps)]
    loads = [pltpu.make_async_copy(r_hbm.at[:, here[n]], r_buf.at[:, here[n]], in_sem.at[n]) for n in range(steps)]
    stores = [pltpu.make_async_copy(buf.at[:, here[n]], out_hbm.at[:, here[n]], sem.at[n]) for n in range(2 * steps)]
    for copy in loads:
        copy.start()
    for n in range(steps):
        loads[n].wait()
        both = dot(w_ref[...], r_buf[:, n * step : (n + 1) * step])
        total = (both[: 2 * count] + both[2 * count :]).astype(BF)
        for h in range(2):
            at = h * half + n * step
            buf[:, at : at + step] = total[h * count : (h + 1) * count]
            stores[h * steps + n].start()
    for copy in stores:
        copy.wait()


def mix(weights, results, steps=4):
    count = weights.shape[0] // 4
    rows, half = results.shape
    hbm = pl.BlockSpec(memory_space=pltpu.HBM)
    return pl.pallas_call(
        functools.partial(mix_body, steps=steps),
        out_shape=jax.ShapeDtypeStruct((count, 2 * half), BF),
        in_specs=[pl.BlockSpec(memory_space=pltpu.VMEM), hbm],
        out_specs=hbm,
        scratch_shapes=[
            pltpu.VMEM((rows, half), BF),
            pltpu.VMEM((count, 2 * half), BF),
            pltpu.SemaphoreType.DMA((steps,)),
            pltpu.SemaphoreType.DMA((2 * steps,)),
        ],
        compiler_params=pltpu.CompilerParams(vmem_limit_bytes=16 * MIB),
        name="mix",
    )(weights, results)


def exchange(x, experts):
    rows, width = x.shape
    x = x.reshape(experts, rows // experts, width)
    return lax.all_to_all(x, AXES, split_axis=0, concat_axis=0, tiled=True).reshape(rows, width)


def on_device(tokens, expert_ids, gate_weights, w_gate, w_up, w_down, gate_scale, up_scale, down_scale):
    experts = lax.axis_size(AXES)
    slots = 4
    ids, weights = expert_ids.T, gate_weights.T
    packed = pack(ids, tokens, experts, slots)
    received = exchange(packed, experts)
    routed = expert(received, w_gate, w_up, w_down, gate_scale, up_scale, down_scale, slots)
    returned = exchange(routed, experts)
    return mix(mixer(ids, weights, experts, slots), returned)


def solution(mesh):
    row = P(AXES, None)
    placed = (row, row, row, P(AXES, None, None), P(AXES, None, None), P(AXES, None, None), row, row, row)
    return jax.shard_map(on_device, mesh=mesh, in_specs=placed, out_specs=row, check_vma=False)
```

```python
import functools

import jax
import jax.numpy as jnp
from jax import lax
from jax.experimental import pallas as pl
from jax.experimental.pallas import tpu as pltpu
from jax.sharding import PartitionSpec as P

AXES = ("node", "wide")
BF = jnp.bfloat16
F32 = jnp.float32
MIB = 1 << 20


def iota(shape, dim):
    return lax.broadcasted_iota(jnp.int32, shape, dim)


def onehot(mask):
    return jnp.where(mask, 1.0, 0.0).astype(BF)


def dot(a, b, dims=((1,), (0,))):
    return lax.dot_general(a, b, (dims, ((), ())), preferred_element_type=F32)


def in_hbm(x):
    return pltpu.with_memory_space_constraint(x, pltpu.HBM)


def codes(ids, experts):
    top, count = ids.shape
    named = jnp.zeros((experts, count), F32)
    for k in range(top):
        named = named + jnp.where(iota((experts, count), 0) == ids[k : k + 1, :], 1.0, 0.0)
    named = named.astype(BF)
    lane = iota((count, 2 * count), 1) % count
    row = iota((count, 2 * count), 0)
    position = dot(named, onehot(row < lane))
    twice = dot(named, onehot(row == lane))
    return (position + 8.0 * (1.0 - twice)).astype(BF)


def pack_body(ids_hbm, tokens_hbm, out_ref, ids_ref, tok_ref, sem, *, experts, slots, steps):
    count, width = tok_ref.shape
    half = width // 2
    rows = experts * 2 * slots
    ids_copy = pltpu.make_async_copy(ids_hbm, ids_ref, sem.at[0])
    tok_copy = pltpu.make_async_copy(tokens_hbm, tok_ref, sem.at[1])
    ids_copy.start()
    tok_copy.start()
    shape = (rows, 2 * count)
    spread = onehot(iota((rows, experts), 0) // (2 * slots) == iota((rows, experts), 1))
    slot = (iota(shape, 0) % slots).astype(F32)
    half_of = iota(shape, 0) // slots % 2 == iota(shape, 1) // count
    ids_copy.wait()
    wide = dot(spread, codes(ids_ref[...], experts))
    hot = onehot((wide == slot) & half_of)
    tok_copy.wait()
    step = half // steps
    for n in range(steps):
        at = slice(n * step, (n + 1) * step)
        stacked = jnp.concatenate([tok_ref[:, at], tok_ref[:, half + n * step : half + (n + 1) * step]], axis=0)
        out_ref[:, at] = dot(hot, stacked).astype(BF)


def pack(ids, tokens, experts, slots, steps=4):
    rows = experts * 2 * slots
    hbm = pl.BlockSpec(memory_space=pltpu.HBM)
    return pl.pallas_call(
        functools.partial(pack_body, experts=experts, slots=slots, steps=steps),
        out_shape=jax.ShapeDtypeStruct((rows, tokens.shape[1] // 2), BF),
        in_specs=[hbm, hbm],
        out_specs=pl.BlockSpec(memory_space=pltpu.VMEM),
        scratch_shapes=[
            pltpu.VMEM(ids.shape, jnp.int32),
            pltpu.VMEM(tokens.shape, BF),
            pltpu.SemaphoreType.DMA((2,)),
        ],
        compiler_params=pltpu.CompilerParams(vmem_limit_bytes=12 * MIB),
        name="pack",
    )(in_hbm(ids), in_hbm(tokens))


def table(ids, weights, experts, slots):
    top, count = ids.shape
    rows = experts * 2 * slots
    code = codes(ids, experts)
    chosen = jnp.zeros((experts, count), F32)
    for k in range(top):
        chosen = chosen + jnp.where(iota((experts, count), 0) == ids[k : k + 1, :], weights[k : k + 1, :], 0.0)
    twice = onehot(iota((count, 2 * count), 0) == iota((count, 2 * count), 1) % count)
    spread = onehot(iota((experts, rows), 1) // (2 * slots) == iota((experts, rows), 0))
    shape = (2 * count, rows)
    wide = dot(code, spread, ((0,), (0,)))
    slot = (iota(shape, 1) % slots).astype(F32)
    here = (wide == slot) & (iota(shape, 1) // slots % 2 == iota(shape, 0) // count)
    high = chosen.astype(BF)
    low = (chosen - high.astype(F32)).astype(BF)
    parts = []
    for part in (high, low):
        part = dot(part, twice).astype(BF)
        part = dot(part, spread, ((0,), (0,)))
        parts.append(jnp.where(here, part, 0.0).astype(BF))
    return jnp.concatenate(parts, axis=0)


def swap(first, second):
    top = iota(first.shape, 1) < 4
    return (
        jnp.where(top, first, pltpu.roll(second, 4, 1)),
        jnp.where(top, pltpu.roll(first, 4, 1), second),
    )


def expert_body(
    x_ref, gate_ref, up_ref, down_hbm, gate_s, up_s, down_s, out_ref, d_buf, xs, hid, d_sem, *, slots, nb, cb
):
    rows, half = x_ref.shape
    ffw = gate_s.shape[1]
    wn, wc = ffw // nb, half // cb
    blocks = rows // 256
    downs = [pltpu.make_async_copy(down_hbm.at[0, pl.ds(n * wn, wn)], d_buf.at[pl.ds(n * wn, wn)], d_sem.at[n]) for n in range(nb)]
    for copy in downs:
        copy.start()
    wx = 256
    for n in range(half // wx):
        at = slice(n * wx, (n + 1) * wx)
        pairs = x_ref[:, at].astype(F32).reshape(rows // 16, 2, 8, wx)
        low, high = swap(pairs[:, 0], pairs[:, 1])
        xs[:, at] = low.reshape(rows // 2, wx).astype(BF)
        xs[:, half + n * wx : half + (n + 1) * wx] = high.reshape(rows // 2, wx).astype(BF)
    for n in range(nb):
        at = slice(n * wn, (n + 1) * wn)
        gate = dot(xs[...], gate_ref[0, :, at]) * gate_s[:, at]
        up = dot(xs[...], up_ref[0, :, at]) * up_s[:, at]
        hid[:, at] = (gate / (1.0 + jnp.exp(-gate)) * up).astype(BF)
    for copy in downs:
        copy.wait()
    for c in range(cb):
        at, to = slice(c * wc, (c + 1) * wc), slice(half + c * wc, half + (c + 1) * wc)
        low = dot(hid[...], d_buf[:, at]) * down_s[:, at]
        high = dot(hid[...], d_buf[:, to]) * down_s[:, to]
        tile = (rows // 16, 8, wc)
        even, odd = swap(low.reshape(tile), high.reshape(tile))
        both = jnp.concatenate([even[:, None], odd[:, None]], axis=1)
        out_ref[:, at] = both.reshape(rows, wc).astype(BF)


def expert(x, w_gate, w_up, w_down, gate_scale, up_scale, down_scale, slots, nb=1, cb=8):
    rows, half = x.shape
    width, ffw = w_gate.shape[1:]
    whole = pl.BlockSpec(memory_space=pltpu.VMEM)
    hbm = pl.BlockSpec(memory_space=pltpu.HBM)
    return pl.pallas_call(
        functools.partial(expert_body, slots=slots, nb=nb, cb=cb),
        out_shape=jax.ShapeDtypeStruct((rows, half), BF),
        in_specs=[whole, whole, whole, hbm, whole, whole, whole],
        out_specs=whole,
        scratch_shapes=[
            pltpu.VMEM((ffw, width), BF),
            pltpu.VMEM((rows // 2, width), BF),
            pltpu.VMEM((rows // 2, ffw), BF),
            pltpu.SemaphoreType.DMA((nb,)),
        ],
        compiler_params=pltpu.CompilerParams(vmem_limit_bytes=20 * MIB),
        name="expert",
    )(x, w_gate, w_up, in_hbm(w_down), gate_scale, up_scale, down_scale)


def mix_body(ids_ref, weights_ref, r_ref, out_hbm, w_ref, buf, sem, *, experts, slots, steps):
    count = ids_ref.shape[1]
    w_ref[...] = table(ids_ref[...], weights_ref[...], experts, slots)
    half = r_ref.shape[1]
    step = half // steps
    here = [pl.ds(n * step, step) for n in range(2 * steps)]
    stores = [pltpu.make_async_copy(buf.at[:, here[n]], out_hbm.at[:, here[n]], sem.at[n]) for n in range(2 * steps)]
    for n in range(steps):
        both = dot(w_ref[...], r_ref[:, n * step : (n + 1) * step])
        total = (both[: 2 * count] + both[2 * count :]).astype(BF)
        for h in range(2):
            at = h * half + n * step
            buf[:, at : at + step] = total[h * count : (h + 1) * count]
            stores[h * steps + n].start()
    for copy in stores:
        copy.wait()


def mix(ids, weights, results, experts, slots, steps=4):
    count = ids.shape[1]
    rows, half = results.shape
    whole = pl.BlockSpec(memory_space=pltpu.VMEM)
    return pl.pallas_call(
        functools.partial(mix_body, experts=experts, slots=slots, steps=steps),
        out_shape=jax.ShapeDtypeStruct((count, 2 * half), BF),
        in_specs=[whole, whole, whole],
        out_specs=pl.BlockSpec(memory_space=pltpu.HBM),
        scratch_shapes=[pltpu.VMEM((4 * count, rows), BF), pltpu.VMEM((count, 2 * half), BF), pltpu.SemaphoreType.DMA((2 * steps,))],
        compiler_params=pltpu.CompilerParams(vmem_limit_bytes=8 * MIB),
        name="mix",
    )(ids, weights, results)


def exchange(x, experts):
    rows, width = x.shape
    x = x.reshape(experts, rows // experts, width)
    return lax.all_to_all(x, AXES, split_axis=0, concat_axis=0, tiled=True).reshape(rows, width)


def on_device(tokens, expert_ids, gate_weights, w_gate, w_up, w_down, gate_scale, up_scale, down_scale):
    experts = lax.axis_size(AXES)
    slots = 4
    ids, weights = expert_ids.T, gate_weights.T
    packed = pack(ids, tokens, experts, slots)
    received = exchange(packed, experts)
    routed = expert(received, w_gate, w_up, w_down, gate_scale, up_scale, down_scale, slots)
    returned = exchange(routed, experts)
    return mix(ids, weights, returned, experts, slots)


def solution(mesh):
    row = P(AXES, None)
    placed = (row, row, row, P(AXES, None, None), P(AXES, None, None), P(AXES, None, None), row, row, row)
    return jax.shard_map(on_device, mesh=mesh, in_specs=placed, out_specs=row, check_vma=False)
```

```python
import functools

import jax
import jax.numpy as jnp
from jax import lax
from jax.experimental import pallas as pl
from jax.experimental.pallas import tpu as pltpu
from jax.sharding import PartitionSpec as P

AXES = ("node", "wide")
BF = jnp.bfloat16
F32 = jnp.float32
MIB = 1 << 20


def iota(shape, dim):
    return lax.broadcasted_iota(jnp.int32, shape, dim)


def onehot(mask):
    return jnp.where(mask, 1.0, 0.0).astype(BF)


def dot(a, b, dims=((1,), (0,))):
    return lax.dot_general(a, b, (dims, ((), ())), preferred_element_type=F32)


def in_hbm(x):
    return pltpu.with_memory_space_constraint(x, pltpu.HBM)


def codes(ids, experts):
    top, count = ids.shape
    named = jnp.zeros((experts, count), F32)
    for k in range(top):
        named = named + jnp.where(iota((experts, count), 0) == ids[k : k + 1, :], 1.0, 0.0)
    named = named.astype(BF)
    lane = iota((count, 2 * count), 1) % count
    row = iota((count, 2 * count), 0)
    position = dot(named, onehot(row < lane))
    twice = dot(named, onehot(row == lane))
    return (position + 8.0 * (1.0 - twice)).astype(BF)


def pack_body(ids_hbm, tokens_hbm, out_ref, ids_ref, tok_ref, sem, *, experts, slots, steps):
    count, width = tok_ref.shape
    half = width // 2
    rows = experts * 2 * slots
    ids_copy = pltpu.make_async_copy(ids_hbm, ids_ref, sem.at[0])
    tok_copy = pltpu.make_async_copy(tokens_hbm, tok_ref, sem.at[1])
    ids_copy.start()
    tok_copy.start()
    shape = (rows, 2 * count)
    spread = onehot(iota((rows, experts), 0) // (2 * slots) == iota((rows, experts), 1))
    slot = (iota(shape, 0) % slots).astype(F32)
    half_of = iota(shape, 0) // slots % 2 == iota(shape, 1) // count
    ids_copy.wait()
    code = codes(ids_ref[...], experts)
    step = rows // 2
    wide = [dot(spread[n * step : (n + 1) * step], code) for n in range(2)]
    hot = [onehot((wide[n] == slot[n * step : (n + 1) * step]) & half_of[n * step : (n + 1) * step]) for n in range(2)]
    tok_copy.wait()
    stacked = jnp.concatenate([tok_ref[:, :half], tok_ref[:, half:]], axis=0)
    for n in range(2):
        out_ref[n * step : (n + 1) * step, :] = dot(hot[n], stacked).astype(BF)


def pack(ids, tokens, experts, slots, steps=4):
    rows = experts * 2 * slots
    hbm = pl.BlockSpec(memory_space=pltpu.HBM)
    return pl.pallas_call(
        functools.partial(pack_body, experts=experts, slots=slots, steps=steps),
        out_shape=jax.ShapeDtypeStruct((rows, tokens.shape[1] // 2), BF),
        in_specs=[hbm, hbm],
        out_specs=pl.BlockSpec(memory_space=pltpu.VMEM),
        scratch_shapes=[
            pltpu.VMEM(ids.shape, jnp.int32),
            pltpu.VMEM(tokens.shape, BF),
            pltpu.SemaphoreType.DMA((2,)),
        ],
        compiler_params=pltpu.CompilerParams(vmem_limit_bytes=12 * MIB),
        name="pack",
    )(in_hbm(ids), in_hbm(tokens))


def table(ids, weights, out_ref, experts, slots):
    top, count = ids.shape
    rows = experts * 2 * slots
    code = codes(ids, experts)
    chosen = jnp.zeros((experts, count), F32)
    for k in range(top):
        chosen = chosen + jnp.where(iota((experts, count), 0) == ids[k : k + 1, :], weights[k : k + 1, :], 0.0)
    high = chosen.astype(BF)
    low = (chosen - high.astype(F32)).astype(BF)
    yield
    twice = onehot(iota((count, 2 * count), 0) == iota((count, 2 * count), 1) % count)
    parts = [dot(part, twice).astype(BF) for part in (high, low)]
    spread = onehot(iota((experts, rows), 1) // (2 * slots) == iota((experts, rows), 0))
    shape = (2 * count, rows)
    yield
    wide = dot(code, spread, ((0,), (0,)))
    slot = (iota(shape, 1) % slots).astype(F32)
    here = (wide == slot) & (iota(shape, 1) // slots % 2 == iota(shape, 0) // count)
    for n, part in enumerate(parts):
        yield
        part = dot(part, spread, ((0,), (0,)))
        out_ref[n * 2 * count : (n + 1) * 2 * count, :] = jnp.where(here, part, 0.0).astype(BF)
    yield


def swap(first, second):
    top = iota(first.shape, 1) < 4
    return (
        jnp.where(top, first, pltpu.roll(second, 4, 1)),
        jnp.where(top, pltpu.roll(first, 4, 1), second),
    )


def expert_body(
    x_ref, gate_ref, up_ref, down_hbm, gate_s, up_s, down_s, ids_ref, weights_ref, out_ref, table_ref, d_buf, xs, hid, d_sem, *, slots, nb, cb
):
    rows, half = x_ref.shape
    ffw = gate_s.shape[1]
    wn, wc = ffw // nb, half // cb
    blocks = rows // 256
    downs = [pltpu.make_async_copy(down_hbm.at[0, pl.ds(n * wn, wn)], d_buf.at[pl.ds(n * wn, wn)], d_sem.at[n]) for n in range(nb)]
    for copy in downs:
        copy.start()
    steps = table(ids_ref[...], weights_ref[...], table_ref, rows // (2 * slots), slots)
    wx = 256
    for n in range(half // wx):
        at = slice(n * wx, (n + 1) * wx)
        pairs = x_ref[:, at].astype(F32).reshape(rows // 16, 2, 8, wx)
        low, high = swap(pairs[:, 0], pairs[:, 1])
        xs[:, at] = low.reshape(rows // 2, wx).astype(BF)
        xs[:, half + n * wx : half + (n + 1) * wx] = high.reshape(rows // 2, wx).astype(BF)
    for n in range(nb):
        at = slice(n * wn, (n + 1) * wn)
        gate = dot(xs[...], gate_ref[0, :, at]) * gate_s[:, at]
        up = dot(xs[...], up_ref[0, :, at]) * up_s[:, at]
        hid[:, at] = (gate / (1.0 + jnp.exp(-gate)) * up).astype(BF)
    for copy in downs:
        copy.wait()
    for c in range(cb):
        next(steps, None)
        at, to = slice(c * wc, (c + 1) * wc), slice(half + c * wc, half + (c + 1) * wc)
        low = dot(hid[...], d_buf[:, at]) * down_s[:, at]
        high = dot(hid[...], d_buf[:, to]) * down_s[:, to]
        tile = (rows // 16, 8, wc)
        even, odd = swap(low.reshape(tile), high.reshape(tile))
        both = jnp.concatenate([even[:, None], odd[:, None]], axis=1)
        out_ref[:, at] = both.reshape(rows, wc).astype(BF)


def expert(x, w_gate, w_up, w_down, gate_scale, up_scale, down_scale, ids, weights, slots, nb=1, cb=8):
    rows, half = x.shape
    width, ffw = w_gate.shape[1:]
    whole = pl.BlockSpec(memory_space=pltpu.VMEM)
    hbm = pl.BlockSpec(memory_space=pltpu.HBM)
    return pl.pallas_call(
        functools.partial(expert_body, slots=slots, nb=nb, cb=cb),
        out_shape=[jax.ShapeDtypeStruct((rows, half), BF), jax.ShapeDtypeStruct((4 * ids.shape[1], rows), BF)],
        in_specs=[whole, whole, whole, hbm] + [whole] * 5,
        out_specs=[whole, whole],
        scratch_shapes=[
            pltpu.VMEM((ffw, width), BF),
            pltpu.VMEM((rows // 2, width), BF),
            pltpu.VMEM((rows // 2, ffw), BF),
            pltpu.SemaphoreType.DMA((nb,)),
        ],
        compiler_params=pltpu.CompilerParams(vmem_limit_bytes=20 * MIB),
        name="expert",
    )(x, w_gate, w_up, in_hbm(w_down), gate_scale, up_scale, down_scale, ids, weights)


def mix_body(w_ref, r_ref, out_hbm, buf, sem, *, steps):
    count = w_ref.shape[0] // 4
    half = r_ref.shape[1]
    step = half // steps
    here = [pl.ds(n * step, step) for n in range(2 * steps)]
    stores = [pltpu.make_async_copy(buf.at[:, here[n]], out_hbm.at[:, here[n]], sem.at[n]) for n in range(2 * steps)]
    for n in range(steps):
        both = dot(w_ref[...], r_ref[:, n * step : (n + 1) * step])
        total = (both[: 2 * count] + both[2 * count :]).astype(BF)
        for h in range(2):
            at = h * half + n * step
            buf[:, at : at + step] = total[h * count : (h + 1) * count]
            stores[h * steps + n].start()
    for copy in stores:
        copy.wait()


def mix(weights, results, steps=4):
    count = weights.shape[0] // 4
    rows, half = results.shape
    whole = pl.BlockSpec(memory_space=pltpu.VMEM)
    return pl.pallas_call(
        functools.partial(mix_body, steps=steps),
        out_shape=jax.ShapeDtypeStruct((count, 2 * half), BF),
        in_specs=[whole, whole],
        out_specs=pl.BlockSpec(memory_space=pltpu.HBM),
        scratch_shapes=[pltpu.VMEM((count, 2 * half), BF), pltpu.SemaphoreType.DMA((2 * steps,))],
        compiler_params=pltpu.CompilerParams(vmem_limit_bytes=8 * MIB),
        name="mix",
    )(weights, results)


def exchange(x, experts):
    rows, width = x.shape
    x = x.reshape(experts, rows // experts, width)
    return lax.all_to_all(x, AXES, split_axis=0, concat_axis=0, tiled=True).reshape(rows, width)


def on_device(tokens, expert_ids, gate_weights, w_gate, w_up, w_down, gate_scale, up_scale, down_scale):
    experts = lax.axis_size(AXES)
    slots = 4
    ids, weights = expert_ids.T, gate_weights.T
    packed = pack(ids, tokens, experts, slots)
    received = exchange(packed, experts)
    scales = (gate_scale, up_scale, down_scale)
    routed, chosen = expert(received, w_gate, w_up, w_down, *scales, ids, weights, slots)
    returned = exchange(routed, experts)
    return mix(chosen, returned)


def solution(mesh):
    row = P(AXES, None)
    placed = (row, row, row, P(AXES, None, None), P(AXES, None, None), P(AXES, None, None), row, row, row)
    return jax.shard_map(on_device, mesh=mesh, in_specs=placed, out_specs=row, check_vma=False)
```

```python
import functools

import jax
import jax.numpy as jnp
from jax import lax
from jax.experimental import pallas as pl
from jax.experimental.pallas import tpu as pltpu
from jax.sharding import PartitionSpec as P

AXES = ("node", "wide")
BF = jnp.bfloat16
F32 = jnp.float32
MIB = 1 << 20


def iota(shape, dim):
    return lax.broadcasted_iota(jnp.int32, shape, dim)


def onehot(mask):
    return jnp.where(mask, 1.0, 0.0).astype(BF)


def dot(a, b, dims=((1,), (0,))):
    return lax.dot_general(a, b, (dims, ((), ())), preferred_element_type=F32)


def in_hbm(x):
    return pltpu.with_memory_space_constraint(x, pltpu.HBM)


def codes(ids, experts):
    top, count = ids.shape
    named = jnp.zeros((experts, count), F32)
    for k in range(top):
        named = named + jnp.where(iota((experts, count), 0) == ids[k : k + 1, :], 1.0, 0.0)
    named = named.astype(BF)
    lane = iota((count, 2 * count), 1) % count
    row = iota((count, 2 * count), 0)
    position = dot(named, onehot(row < lane))
    twice = dot(named, onehot(row == lane))
    return (position + 8.0 * (1.0 - twice)).astype(BF)


def pack_body(ids_hbm, tokens_hbm, out_ref, ids_ref, tok_ref, sem, *, experts, slots, steps):
    count, width = tok_ref.shape
    half = width // 2
    rows = experts * 2 * slots
    ids_copy = pltpu.make_async_copy(ids_hbm, ids_ref, sem.at[0])
    tok_copy = pltpu.make_async_copy(tokens_hbm, tok_ref, sem.at[1])
    ids_copy.start()
    tok_copy.start()
    shape = (rows, 2 * count)
    spread = onehot(iota((rows, experts), 0) // (2 * slots) == iota((rows, experts), 1))
    slot = (iota(shape, 0) % slots).astype(F32)
    half_of = iota(shape, 0) // slots % 2 == iota(shape, 1) // count
    ids_copy.wait()
    code = codes(ids_ref[...], experts)
    step = rows // 2
    wide = [dot(spread[n * step : (n + 1) * step], code) for n in range(2)]
    hot = [onehot((wide[n] == slot[n * step : (n + 1) * step]) & half_of[n * step : (n + 1) * step]) for n in range(2)]
    tok_copy.wait()
    stacked = jnp.concatenate([tok_ref[:, :half], tok_ref[:, half:]], axis=0)
    for n in range(2):
        out_ref[n * step : (n + 1) * step, :] = dot(hot[n], stacked).astype(BF)


def pack(ids, tokens, experts, slots, steps=4):
    rows = experts * 2 * slots
    hbm = pl.BlockSpec(memory_space=pltpu.HBM)
    return pl.pallas_call(
        functools.partial(pack_body, experts=experts, slots=slots, steps=steps),
        out_shape=jax.ShapeDtypeStruct((rows, tokens.shape[1] // 2), BF),
        in_specs=[hbm, hbm],
        out_specs=pl.BlockSpec(memory_space=pltpu.VMEM),
        scratch_shapes=[
            pltpu.VMEM(ids.shape, jnp.int32),
            pltpu.VMEM(tokens.shape, BF),
            pltpu.SemaphoreType.DMA((2,)),
        ],
        compiler_params=pltpu.CompilerParams(vmem_limit_bytes=12 * MIB),
        name="pack",
    )(in_hbm(ids), in_hbm(tokens))


def table(ids, weights, out_ref, experts, slots):
    top, count = ids.shape
    rows = experts * 2 * slots
    shape = (count, rows)
    named = jnp.zeros((experts, count), F32)
    chosen = jnp.zeros((experts, count), F32)
    for k in range(top):
        here = iota((experts, count), 0) == ids[k : k + 1, :]
        named = jnp.where(here, 1.0, named)
        chosen = jnp.where(here, weights[k : k + 1, :], chosen)
    before = onehot(iota((count, count), 0) < iota((count, count), 1))
    code = (dot(named.astype(BF), before) + 8.0 * (1.0 - named)).astype(BF)
    high = chosen.astype(BF)
    low = (chosen - high.astype(F32)).astype(BF)
    spread = onehot(iota((experts, rows), 1) // (2 * slots) == iota((experts, rows), 0))
    yield
    wide = dot(code, spread, ((0,), (0,)))
    here = wide == (iota(shape, 1) % slots).astype(F32)
    second = iota(shape, 1) // slots % 2 == 1
    for n, part in enumerate((high, low)):
        yield
        part = jnp.where(here, dot(part, spread, ((0,), (0,))), 0.0)
        at = 2 * n * count
        out_ref[at : at + count, :] = jnp.where(second, 0.0, part).astype(BF)
        out_ref[at + count : at + 2 * count, :] = jnp.where(second, part, 0.0).astype(BF)
    yield


def swap(first, second):
    top = iota(first.shape, 1) < 4
    return (
        jnp.where(top, first, pltpu.roll(second, 4, 1)),
        jnp.where(top, pltpu.roll(first, 4, 1), second),
    )


def expert_body(
    x_ref, gate_ref, up_ref, down_hbm, gate_s, up_s, down_s, ids_ref, weights_ref, out_ref, table_ref, d_buf, xs, hid, d_sem, *, slots, nb, cb
):
    rows, half = x_ref.shape
    ffw = gate_s.shape[1]
    wn, wc = ffw // nb, half // cb
    blocks = rows // 256
    downs = [pltpu.make_async_copy(down_hbm.at[0, pl.ds(n * wn, wn)], d_buf.at[pl.ds(n * wn, wn)], d_sem.at[n]) for n in range(nb)]
    for copy in downs:
        copy.start()
    steps = table(ids_ref[...], weights_ref[...], table_ref, rows // (2 * slots), slots)
    wx = 256
    for n in range(half // wx):
        at = slice(n * wx, (n + 1) * wx)
        pairs = x_ref[:, at].astype(F32).reshape(rows // 16, 2, 8, wx)
        low, high = swap(pairs[:, 0], pairs[:, 1])
        xs[:, at] = low.reshape(rows // 2, wx).astype(BF)
        xs[:, half + n * wx : half + (n + 1) * wx] = high.reshape(rows // 2, wx).astype(BF)
    for n in range(nb):
        at = slice(n * wn, (n + 1) * wn)
        gate = dot(xs[...], gate_ref[0, :, at]) * gate_s[:, at]
        up = dot(xs[...], up_ref[0, :, at]) * up_s[:, at]
        hid[:, at] = (gate / (1.0 + jnp.exp(-gate)) * up).astype(BF)
    for copy in downs:
        copy.wait()
    for c in range(cb):
        next(steps, None)
        at, to = slice(c * wc, (c + 1) * wc), slice(half + c * wc, half + (c + 1) * wc)
        low = dot(hid[...], d_buf[:, at]) * down_s[:, at]
        high = dot(hid[...], d_buf[:, to]) * down_s[:, to]
        tile = (rows // 16, 8, wc)
        even, odd = swap(low.reshape(tile), high.reshape(tile))
        both = jnp.concatenate([even[:, None], odd[:, None]], axis=1)
        out_ref[:, at] = both.reshape(rows, wc).astype(BF)


def expert(x, w_gate, w_up, w_down, gate_scale, up_scale, down_scale, ids, weights, slots, nb=1, cb=8):
    rows, half = x.shape
    width, ffw = w_gate.shape[1:]
    whole = pl.BlockSpec(memory_space=pltpu.VMEM)
    hbm = pl.BlockSpec(memory_space=pltpu.HBM)
    return pl.pallas_call(
        functools.partial(expert_body, slots=slots, nb=nb, cb=cb),
        out_shape=[jax.ShapeDtypeStruct((rows, half), BF), jax.ShapeDtypeStruct((4 * ids.shape[1], rows), BF)],
        in_specs=[whole, whole, whole, hbm] + [whole] * 5,
        out_specs=[whole, whole],
        scratch_shapes=[
            pltpu.VMEM((ffw, width), BF),
            pltpu.VMEM((rows // 2, width), BF),
            pltpu.VMEM((rows // 2, ffw), BF),
            pltpu.SemaphoreType.DMA((nb,)),
        ],
        compiler_params=pltpu.CompilerParams(vmem_limit_bytes=20 * MIB),
        name="expert",
    )(x, w_gate, w_up, in_hbm(w_down), gate_scale, up_scale, down_scale, ids, weights)


def mix_body(w_ref, r_ref, out_hbm, buf, sem, *, steps):
    count = w_ref.shape[0] // 4
    half = r_ref.shape[1]
    step = half // steps
    here = [pl.ds(n * step, step) for n in range(2 * steps)]
    stores = [pltpu.make_async_copy(buf.at[:, here[n]], out_hbm.at[:, here[n]], sem.at[n]) for n in range(2 * steps)]
    for n in range(steps):
        both = dot(w_ref[...], r_ref[:, n * step : (n + 1) * step])
        total = (both[: 2 * count] + both[2 * count :]).astype(BF)
        for h in range(2):
            at = h * half + n * step
            buf[:, at : at + step] = total[h * count : (h + 1) * count]
            stores[h * steps + n].start()
    for copy in stores:
        copy.wait()


def mix(weights, results, steps=4):
    count = weights.shape[0] // 4
    rows, half = results.shape
    whole = pl.BlockSpec(memory_space=pltpu.VMEM)
    return pl.pallas_call(
        functools.partial(mix_body, steps=steps),
        out_shape=jax.ShapeDtypeStruct((count, 2 * half), BF),
        in_specs=[whole, whole],
        out_specs=pl.BlockSpec(memory_space=pltpu.HBM),
        scratch_shapes=[pltpu.VMEM((count, 2 * half), BF), pltpu.SemaphoreType.DMA((2 * steps,))],
        compiler_params=pltpu.CompilerParams(vmem_limit_bytes=8 * MIB),
        name="mix",
    )(weights, results)


def exchange(x, experts):
    rows, width = x.shape
    x = x.reshape(experts, rows // experts, width)
    return lax.all_to_all(x, AXES, split_axis=0, concat_axis=0, tiled=True).reshape(rows, width)


def on_device(tokens, expert_ids, gate_weights, w_gate, w_up, w_down, gate_scale, up_scale, down_scale):
    experts = lax.axis_size(AXES)
    slots = 4
    ids, weights = expert_ids.T, gate_weights.T
    packed = pack(ids, tokens, experts, slots)
    received = exchange(packed, experts)
    scales = (gate_scale, up_scale, down_scale)
    routed, chosen = expert(received, w_gate, w_up, w_down, *scales, ids, weights, slots)
    returned = exchange(routed, experts)
    return mix(chosen, returned)


def solution(mesh):
    row = P(AXES, None)
    placed = (row, row, row, P(AXES, None, None), P(AXES, None, None), P(AXES, None, None), row, row, row)
    return jax.shard_map(on_device, mesh=mesh, in_specs=placed, out_specs=row, check_vma=False)
```

```python
import functools

import jax
import jax.numpy as jnp
from jax import lax
from jax.experimental import pallas as pl
from jax.experimental.pallas import tpu as pltpu
from jax.sharding import PartitionSpec as P

AXES = ("node", "wide")
BF = jnp.bfloat16
F32 = jnp.float32
MIB = 1 << 20


def iota(shape, dim):
    return lax.broadcasted_iota(jnp.int32, shape, dim)


def onehot(mask):
    return jnp.where(mask, 1.0, 0.0).astype(BF)


def dot(a, b, dims=((1,), (0,))):
    return lax.dot_general(a, b, (dims, ((), ())), preferred_element_type=F32)


def in_hbm(x):
    return pltpu.with_memory_space_constraint(x, pltpu.HBM)


def codes(ids, experts):
    top, count = ids.shape
    named = jnp.zeros((experts, count), F32)
    for k in range(top):
        named = named + jnp.where(iota((experts, count), 0) == ids[k : k + 1, :], 1.0, 0.0)
    named = named.astype(BF)
    lane = iota((count, 2 * count), 1) % count
    row = iota((count, 2 * count), 0)
    position = dot(named, onehot(row < lane))
    twice = dot(named, onehot(row == lane))
    return (position + 8.0 * (1.0 - twice)).astype(BF)


def pack_body(ids_hbm, tokens_hbm, out_ref, ids_ref, tok_ref, sem, *, experts, slots, steps):
    count, width = tok_ref.shape
    half = width // 2
    rows = experts * 2 * slots
    ids_copy = pltpu.make_async_copy(ids_hbm, ids_ref, sem.at[0])
    tok_copy = pltpu.make_async_copy(tokens_hbm, tok_ref, sem.at[1])
    ids_copy.start()
    tok_copy.start()
    shape = (rows, 2 * count)
    spread = onehot(iota((rows, experts), 0) // (2 * slots) == iota((rows, experts), 1))
    slot = (iota(shape, 0) % slots).astype(F32)
    half_of = iota(shape, 0) // slots % 2 == iota(shape, 1) // count
    ids_copy.wait()
    code = codes(ids_ref[...], experts)
    step = rows // 2
    wide = [dot(spread[n * step : (n + 1) * step], code) for n in range(2)]
    hot = [onehot((wide[n] == slot[n * step : (n + 1) * step]) & half_of[n * step : (n + 1) * step]) for n in range(2)]
    tok_copy.wait()
    stacked = jnp.concatenate([tok_ref[:, :half], tok_ref[:, half:]], axis=0)
    for n in range(2):
        out_ref[n * step : (n + 1) * step, :] = dot(hot[n], stacked).astype(BF)


def pack(ids, tokens, experts, slots, steps=4):
    rows = experts * 2 * slots
    hbm = pl.BlockSpec(memory_space=pltpu.HBM)
    return pl.pallas_call(
        functools.partial(pack_body, experts=experts, slots=slots, steps=steps),
        out_shape=jax.ShapeDtypeStruct((rows, tokens.shape[1] // 2), BF),
        in_specs=[hbm, hbm],
        out_specs=pl.BlockSpec(memory_space=pltpu.VMEM),
        scratch_shapes=[
            pltpu.VMEM(ids.shape, jnp.int32),
            pltpu.VMEM(tokens.shape, BF),
            pltpu.SemaphoreType.DMA((2,)),
        ],
        compiler_params=pltpu.CompilerParams(vmem_limit_bytes=12 * MIB),
        name="pack",
    )(in_hbm(ids), in_hbm(tokens))


def table(ids, weights, out_ref, experts, slots):
    top, count = ids.shape
    rows = experts * 2 * slots
    shape = (count, rows)
    named = jnp.zeros((experts, count), F32)
    chosen = jnp.zeros((experts, count), F32)
    for k in range(top):
        here = iota((experts, count), 0) == ids[k : k + 1, :]
        named = jnp.where(here, 1.0, named)
        chosen = jnp.where(here, weights[k : k + 1, :], chosen)
    before = onehot(iota((count, count), 0) < iota((count, count), 1))
    code = (dot(named.astype(BF), before) + 8.0 * (1.0 - named)).astype(BF)
    high = chosen.astype(BF)
    low = (chosen - high.astype(F32)).astype(BF)
    spread = onehot(iota((experts, rows), 1) // (2 * slots) == iota((experts, rows), 0))
    yield
    wide = dot(code, spread, ((0,), (0,)))
    here = wide == (iota(shape, 1) % slots).astype(F32)
    second = iota(shape, 1) // slots % 2 == 1
    for n, part in enumerate((high, low)):
        yield
        part = jnp.where(here, dot(part, spread, ((0,), (0,))), 0.0)
        at = 2 * n * count
        out_ref[at : at + count, :] = jnp.where(second, 0.0, part).astype(BF)
        out_ref[at + count : at + 2 * count, :] = jnp.where(second, part, 0.0).astype(BF)
    yield


def swap(first, second):
    top = iota(first.shape, 1) < 4
    return (
        jnp.where(top, first, pltpu.roll(second, 4, 1)),
        jnp.where(top, pltpu.roll(first, 4, 1), second),
    )


def expert_body(
    x_ref, gate_ref, up_ref, down_hbm, gate_s, up_s, down_s, ids_ref, weights_ref, out_ref, table_ref, d_buf, xs, hid, d_sem, *, slots, nb, cb
):
    rows, half = x_ref.shape
    ffw = gate_s.shape[1]
    wn, wc = ffw // nb, half // cb
    blocks = rows // 256
    downs = [pltpu.make_async_copy(down_hbm.at[0, pl.ds(n * wn, wn)], d_buf.at[pl.ds(n * wn, wn)], d_sem.at[n]) for n in range(nb)]
    for copy in downs:
        copy.start()
    steps = table(ids_ref[...], weights_ref[...], table_ref, rows // (2 * slots), slots)
    wx = 256
    gate = None
    for g in range(2):
        for n in range(g * half // wx // 2, (g + 1) * half // wx // 2):
            at = slice(n * wx, (n + 1) * wx)
            pairs = x_ref[:, at].astype(F32).reshape(rows // 16, 2, 8, wx)
            low, high = swap(pairs[:, 0], pairs[:, 1])
            xs[:, at] = low.reshape(rows // 2, wx).astype(BF)
            xs[:, half + n * wx : half + (n + 1) * wx] = high.reshape(rows // 2, wx).astype(BF)
        for h in range(2):
            at = slice(h * half + g * half // 2, h * half + (g + 1) * half // 2)
            part = dot(xs[:, at], gate_ref[0, at, :])
            gate = part if gate is None else gate + part
    gate = gate * gate_s[...]
    up = dot(xs[...], up_ref[0]) * up_s[...]
    hid[...] = (gate / (1.0 + jnp.exp(-gate)) * up).astype(BF)
    for copy in downs:
        copy.wait()
    for c in range(cb):
        next(steps, None)
        at, to = slice(c * wc, (c + 1) * wc), slice(half + c * wc, half + (c + 1) * wc)
        low = dot(hid[...], d_buf[:, at]) * down_s[:, at]
        high = dot(hid[...], d_buf[:, to]) * down_s[:, to]
        tile = (rows // 16, 8, wc)
        even, odd = swap(low.reshape(tile), high.reshape(tile))
        both = jnp.concatenate([even[:, None], odd[:, None]], axis=1)
        out_ref[:, at] = both.reshape(rows, wc).astype(BF)


def expert(x, w_gate, w_up, w_down, gate_scale, up_scale, down_scale, ids, weights, slots, nb=1, cb=8):
    rows, half = x.shape
    width, ffw = w_gate.shape[1:]
    whole = pl.BlockSpec(memory_space=pltpu.VMEM)
    hbm = pl.BlockSpec(memory_space=pltpu.HBM)
    return pl.pallas_call(
        functools.partial(expert_body, slots=slots, nb=nb, cb=cb),
        out_shape=[jax.ShapeDtypeStruct((rows, half), BF), jax.ShapeDtypeStruct((4 * ids.shape[1], rows), BF)],
        in_specs=[whole, whole, whole, hbm] + [whole] * 5,
        out_specs=[whole, whole],
        scratch_shapes=[
            pltpu.VMEM((ffw, width), BF),
            pltpu.VMEM((rows // 2, width), BF),
            pltpu.VMEM((rows // 2, ffw), BF),
            pltpu.SemaphoreType.DMA((nb,)),
        ],
        compiler_params=pltpu.CompilerParams(vmem_limit_bytes=20 * MIB),
        name="expert",
    )(x, w_gate, w_up, in_hbm(w_down), gate_scale, up_scale, down_scale, ids, weights)


def mix_body(w_ref, r_ref, out_hbm, buf, sem, *, steps):
    count = w_ref.shape[0] // 4
    half = r_ref.shape[1]
    step = half // steps
    here = [pl.ds(n * step, step) for n in range(2 * steps)]
    stores = [pltpu.make_async_copy(buf.at[:, here[n]], out_hbm.at[:, here[n]], sem.at[n]) for n in range(2 * steps)]
    for n in range(steps):
        both = dot(w_ref[...], r_ref[:, n * step : (n + 1) * step])
        total = (both[: 2 * count] + both[2 * count :]).astype(BF)
        for h in range(2):
            at = h * half + n * step
            buf[:, at : at + step] = total[h * count : (h + 1) * count]
            stores[h * steps + n].start()
    for copy in stores:
        copy.wait()


def mix(weights, results, steps=4):
    count = weights.shape[0] // 4
    rows, half = results.shape
    whole = pl.BlockSpec(memory_space=pltpu.VMEM)
    return pl.pallas_call(
        functools.partial(mix_body, steps=steps),
        out_shape=jax.ShapeDtypeStruct((count, 2 * half), BF),
        in_specs=[whole, whole],
        out_specs=pl.BlockSpec(memory_space=pltpu.HBM),
        scratch_shapes=[pltpu.VMEM((count, 2 * half), BF), pltpu.SemaphoreType.DMA((2 * steps,))],
        compiler_params=pltpu.CompilerParams(vmem_limit_bytes=8 * MIB),
        name="mix",
    )(weights, results)


def exchange(x, experts):
    rows, width = x.shape
    x = x.reshape(experts, rows // experts, width)
    return lax.all_to_all(x, AXES, split_axis=0, concat_axis=0, tiled=True).reshape(rows, width)


def on_device(tokens, expert_ids, gate_weights, w_gate, w_up, w_down, gate_scale, up_scale, down_scale):
    experts = lax.axis_size(AXES)
    slots = 4
    ids, weights = expert_ids.T, gate_weights.T
    packed = pack(ids, tokens, experts, slots)
    received = exchange(packed, experts)
    scales = (gate_scale, up_scale, down_scale)
    routed, chosen = expert(received, w_gate, w_up, w_down, *scales, ids, weights, slots)
    returned = exchange(routed, experts)
    return mix(chosen, returned)


def solution(mesh):
    row = P(AXES, None)
    placed = (row, row, row, P(AXES, None, None), P(AXES, None, None), P(AXES, None, None), row, row, row)
    return jax.shard_map(on_device, mesh=mesh, in_specs=placed, out_specs=row, check_vma=False)
```
